32 devices in a mesh: dp: 8 (over y, x, core), tensor: 4 (over z).
Axes of the slice: x: 2, y: 2, z: 4, core: 2. Of those that a mesh axis runs over, the one named last changes fastest.
Arguments:
- tokens: bfloat16 [4096, 2048], P(('dp', 'tensor')), may hold values from -6 to 6
- cotangent: bfloat16 [4096, 2048], P(('dp', 'tensor')), may hold values from -6 to 6
- segments: int32 [4096], P('dp'), may hold values from 0 to 2, as said below
- positions: int32 [4096], P('dp'), may hold values from 0 to 1535, as said below
- norm_gain: bfloat16 [1, 2, 2048], P(None, None, 'dp'), may hold values from 0.5 to 1.5
- norm_bias: bfloat16 [1, 2, 2048], P(None, None, 'dp'), may hold values from -1.5 to 1.5
- qkv_weight: bfloat16 [1, 3, 2048, 2048], P(None, None, 'dp', 'tensor'), may hold values from -2 to 2
- qkv_bias: bfloat16 [1, 3, 8, 256], P(None, None, 'tensor', 'dp'), may hold values from -1.5 to 1.5
- dense_weight: bfloat16 [1, 2048, 2048], P(None, 'tensor', 'dp'), may hold values from -0.5 to 0.5
- dense_bias: bfloat16 [1, 2048], P(None, 'dp'), may hold values from -1.5 to 1.5
- in_weight: bfloat16 [1, 2048, 8192], P(None, 'dp', 'tensor'), may hold values from -0.125 to 0.125
- in_bias: bfloat16 [1, 32, 256], P(None, 'tensor', 'dp'), may hold values from -2.5 to 2.5
- out_weight: bfloat16 [1, 8192, 2048], P(None, 'tensor', 'dp'), may hold values from -0.0625 to 0.0625
- out_bias: bfloat16 [1, 2048], P(None, 'dp'), may hold values from -1.5 to 1.5
Outputs:
- layer_out: bfloat16 [4096, 2048], P(('dp', 'tensor'))
- tokens_grad: bfloat16 [4096, 2048], P(('dp', 'tensor'))
- norm_gain_grad: float32 [1, 2, 2048], P(None, None, 'dp')
- norm_bias_grad: float32 [1, 2, 2048], P(None, None, 'dp')
- qkv_weight_grad: float32 [1, 3, 2048, 2048], P(None, None, 'dp', 'tensor')
- qkv_bias_grad: float32 [1, 3, 8, 256], P(None, None, 'tensor', 'dp')
- dense_weight_grad: float32 [1, 2048, 2048], P(None, 'tensor', 'dp')
- dense_bias_grad: float32 [1, 2048], P(None, 'dp')
- in_weight_grad: float32 [1, 2048, 8192], P(None, 'dp', 'tensor')
- in_bias_grad: float32 [1, 32, 256], P(None, 'tensor', 'dp')
- out_weight_grad: float32 [1, 8192, 2048], P(None, 'tensor', 'dp')
- out_bias_grad: float32 [1, 2048], P(None, 'dp')
The draws below stay inside these ranges and needn't reach their ends.
Inputs may be any that keep to these rules, and one draw needn't show every extreme that they name: `segments`: within each sequence of 512 tokens the numbers start at 0, never fall and rise by one where a document starts; the first sequence holds three documents. `positions`: positions rise by one a token within a document; the document that opens a sequence may start at any position and ends at or below 1535, every other starts at 0.
All inputs are finite; a program needn't handle non-finite values.
Results may differ from the reference program's by a relative error of at most 0.0092.
Values may be sent and summed in bfloat16 or wider, within the bound.
No kernel may reach another device: no remote copies, remote signals or barrier semaphores. Data moves between devices by JAX's collectives and lax.ppermute only.
A program may use at most 192 MiB of HBM per device.

```python
import math
import jax
import jax.numpy as jnp
from jax import lax

D = 2048
H = 8
HD = 256
ROT = 64
FF = 8192
LAYERS = 1
SEQ = 512
SEQ_DEV = 1
TOKENS = 4096
N_DP = 8


def doc_layout(key):
    seq_count = TOKENS // SEQ
    subkeys = jax.random.split(jax.random.fold_in(key, 7), 5)
    start_one = jax.random.randint(subkeys[0], (seq_count,), SEQ // 8, 5 * SEQ // 8)
    start_lead = jax.random.randint(subkeys[1], (seq_count,), SEQ // 8, SEQ // 4)
    length_two = jax.random.randint(subkeys[2], (seq_count,), 2 * SEQ // 5, 4 * SEQ)
    length_lead = jax.random.randint(subkeys[3], (seq_count,), 2 * SEQ // 5, SEQ // 2)
    offset = jax.random.randint(subkeys[4], (seq_count,), 0, 3 * SEQ)
    leading = jnp.arange(seq_count) == 0
    bound_one = jnp.where(leading, start_lead, start_one)
    bound_two = bound_one + jnp.where(leading, length_lead, length_two)
    offset = jnp.where(leading, 3 * SEQ - bound_one, jnp.minimum(offset, 3 * SEQ - bound_one))
    order = jnp.arange(SEQ, dtype=jnp.int32)[None, :]
    segment = (order >= bound_one[:, None]).astype(jnp.int32) + (order >= bound_two[:, None]).astype(jnp.int32)
    place = jnp.where(segment == 0, order + offset[:, None], jnp.where(segment == 1, order - bound_one[:, None], order - bound_two[:, None]))
    return (segment.reshape(TOKENS).astype(jnp.int32), place.reshape(TOKENS).astype(jnp.int32))


def draw_segments(key, part):
    return doc_layout(key)[0]


def draw_positions(key, part):
    return doc_layout(key)[1]


def draw_qkv_weight(key, part):
    subkeys = jax.random.split(jax.random.fold_in(key, 11), 3)
    shape = (LAYERS, D, D)
    scaling = 1.0 / math.sqrt(D)
    shared = jax.random.truncated_normal(subkeys[0], -4.0, 4.0, shape, jnp.float32)
    spread = jax.random.truncated_normal(subkeys[1], -4.0, 4.0, shape, jnp.float32)
    valued = jax.random.truncated_normal(subkeys[2], -4.0, 4.0, shape, jnp.float32)
    query_part = scaling * shared
    key_part = scaling * spread
    return jnp.stack([query_part, key_part, scaling * valued], axis=1).astype(jnp.bfloat16)


def levels(key, extent, pieces, low, largest):
    def one(axis_at, shards_of):
        heights = jax.random.uniform(jax.random.fold_in(jax.random.fold_in(key, 6), axis_at), (shards_of,), jnp.float32, low / len(pieces), largest / len(pieces))
        return jnp.repeat(jnp.exp(heights), extent[axis_at] // shards_of).reshape((-1,) + (1,) * (len(extent) - axis_at - 1))

    level = one(*pieces[0])
    for cut in pieces[1:]:
        level = level * one(*cut)
    return level


def noise(own_key, dims, width, bound, cuts=(), kind=jnp.bfloat16):
    entries = jax.random.normal(own_key, dims, jnp.float32) * width
    if len(cuts) > 0:
        entries = levels(own_key, dims, cuts, -0.22, 0.18) * entries
    return jnp.clip(entries, min=-bound, max=bound).astype(kind)


def setup_inputs(seed: int = 0) -> dict:
    streams_of = jax.random.split(jax.random.key(seed), 15)
    return {
        "tokens": noise(streams_of[0], (TOKENS, D), 1.0, 6.0, ((0, 32),)),
        "cotangent": noise(streams_of[1], (TOKENS, D), 1.0, 6.0, ((0, 32),)),
        "segments": draw_segments(jax.random.fold_in(streams_of[14], 71), 0),
        "positions": draw_positions(jax.random.fold_in(streams_of[14], 71), 0),
        "norm_gain": jnp.clip(1.0 + 0.1 * jax.random.normal(streams_of[4], (LAYERS, 2, D), jnp.float32), 0.5, 1.5).astype(jnp.bfloat16),
        "norm_bias": noise(streams_of[5], (LAYERS, 2, D), 0.3, 1.5, ((2, 8),)),
        "qkv_weight": draw_qkv_weight(jax.random.fold_in(streams_of[14], 71), 0),
        "qkv_bias": noise(streams_of[7], (LAYERS, 3, H, HD), 0.3, 1.5, ((2, 4), (3, 8))),
        "dense_weight": noise(streams_of[8], (LAYERS, D, D), (D // 16) ** -0.5, 0.5, ((1, 4), (2, 8))),
        "dense_bias": noise(streams_of[9], (LAYERS, D), 0.3, 1.5, ((1, 8),)),
        "in_weight": noise(streams_of[10], (LAYERS, D, FF), D ** -0.5, 0.125, ((1, 8), (2, 4))),
        "in_bias": noise(streams_of[11], (LAYERS, FF // HD, HD), 0.5, 2.5, ((1, 4), (2, 8))),
        "out_weight": noise(streams_of[12], (LAYERS, FF, D), FF ** -0.5, 0.0625, ((1, 4), (2, 8))),
        "out_bias": noise(streams_of[13], (LAYERS, D), 0.3, 1.5, ((1, 8),)),
    }


norm_eps = 1e-05
root_half = 0.7071067811865476
inv_root_tau = 0.3989422804014327

def widen(value_rows):
    return lax.optimization_barrier(value_rows).astype(jnp.float32)

def rope_tables(positions):
    half_rot = ROT // 2
    freq = jnp.exp(jnp.arange(half_rot, dtype=jnp.float32) * (-2.0 * math.log(10000.0) / ROT))
    angle = positions.astype(jnp.float32)[:, None] * freq[None, :]
    return (jnp.cos(angle), jnp.sin(angle))

def rotate(value_rows, cosine, sine, sign):
    half_rot = ROT // 2
    first_half = value_rows[..., :half_rot]
    second_half = value_rows[..., half_rot:ROT]
    cos_wide = cosine[:, None, :]
    sin_wide = sign * sine[:, None, :]
    return jnp.concatenate([first_half * cos_wide - second_half * sin_wide, second_half * cos_wide + first_half * sin_wide, value_rows[..., ROT:]], axis=-1)

def apply_layer_norm(residual_stream):
    centred = residual_stream - lax.optimization_barrier(jnp.mean(residual_stream, axis=-1, keepdims=True))
    reciprocal_deviation = lax.rsqrt(lax.optimization_barrier(jnp.mean(centred * centred, axis=-1, keepdims=True)) + norm_eps)
    return (centred * reciprocal_deviation, reciprocal_deviation)

def build_allowed(segments):
    blocks = segments.reshape(-1, SEQ)
    order = jnp.arange(SEQ)
    causal = order[:, None] >= order[None, :]
    return (blocks[:, :, None] == blocks[:, None, :]) & causal[None]

def gelu(preactivation):
    return 0.5 * preactivation * (1.0 + lax.erf(preactivation * root_half))

def gelu_slope(preactivation):
    return 0.5 * (1.0 + lax.erf(preactivation * root_half)) + preactivation * jnp.exp(-0.5 * preactivation * preactivation) * inv_root_tau

def attend(query_rows, key_rows, value_rows, allowed):
    scaling = 1.0 / math.sqrt(HD)
    scores = jnp.einsum('sqhd,skhd->shqk', widen(query_rows), widen(key_rows)) * scaling
    scores = jnp.where(allowed[:, None], scores, -1e+30)
    top = lax.optimization_barrier(jnp.max(scores, axis=-1, keepdims=True))
    expo = jnp.exp(scores - top)
    total = lax.optimization_barrier(jnp.sum(expo, axis=-1, keepdims=True))
    probs = expo / total
    log_sum_exp = (top + jnp.log(total))[..., 0]
    result_output = jnp.einsum('shqk,skhd->sqhd', widen(probs.astype(jnp.bfloat16)), widen(value_rows)).astype(jnp.bfloat16)
    return (result_output, log_sum_exp)

def attend_back(query_rows, key_rows, value_rows, result_output, log_sum_exp, out_grad, allowed):
    scaling = 1.0 / math.sqrt(HD)
    scores = jnp.einsum('sqhd,skhd->shqk', widen(query_rows), widen(key_rows)) * scaling
    scores = jnp.where(allowed[:, None], scores, -1e+30)
    probs = jnp.exp(scores - log_sum_exp[..., None])
    probs_low = widen(probs.astype(jnp.bfloat16))
    grad_wide = widen(out_grad)
    value_grad = jnp.einsum('shqk,sqhd->skhd', probs_low, grad_wide)
    prob_grad = jnp.einsum('sqhd,skhd->shqk', grad_wide, widen(value_rows))
    delta = jnp.einsum('sqhd,sqhd->shq', grad_wide, widen(result_output))
    score_grad = widen((probs * (prob_grad - delta[..., None])).astype(jnp.bfloat16))
    query_grad = jnp.einsum('shqk,skhd->sqhd', score_grad, widen(key_rows)) * scaling
    key_grad = jnp.einsum('shqk,sqhd->skhd', score_grad, widen(query_rows)) * scaling
    return (query_grad, key_grad, value_grad)

def forward_layer(residual_stream, params, cosine, sine, allowed):
    gain_vectors, shift_vectors, qkv_w, qkv_b, dense_w, dense_b, in_w, in_b, out_w, out_b = params
    count = residual_stream.shape[0]
    groups = count // SEQ
    centered_scaled, reciprocal_deviation = apply_layer_norm(residual_stream)
    norm_output = (centered_scaled[None] * gain_vectors.astype(jnp.float32)[:, None, :] + shift_vectors.astype(jnp.float32)[:, None, :]).astype(jnp.bfloat16)
    proj = jnp.stack([jnp.dot(norm_output[0], qkv_w[part], preferred_element_type=jnp.float32) for part in range(3)])
    proj = proj + qkv_b.reshape(3, 1, D).astype(jnp.float32)
    shaped = proj.reshape(3, count, H, HD)
    query_rows = rotate(shaped[0], cosine, sine, 1.0).astype(jnp.bfloat16).reshape(groups, SEQ, H, HD)
    key_rows = rotate(shaped[1], cosine, sine, 1.0).astype(jnp.bfloat16).reshape(groups, SEQ, H, HD)
    value_rows = shaped[2].astype(jnp.bfloat16).reshape(groups, SEQ, H, HD)
    result_output, log_sum_exp = attend(query_rows, key_rows, value_rows, allowed)
    flat = result_output.reshape(count, D)
    preactivation = jnp.dot(norm_output[1], in_w, preferred_element_type=jnp.float32) + in_b.reshape(FF).astype(jnp.float32)
    activation_value = gelu(preactivation).astype(jnp.bfloat16)
    attn_branch = jnp.dot(flat, dense_w, preferred_element_type=jnp.float32)
    mlp_branch = jnp.dot(activation_value, out_w, preferred_element_type=jnp.float32)
    updated_residual = residual_stream + attn_branch + mlp_branch + dense_b.astype(jnp.float32) + out_b.astype(jnp.float32)
    return (updated_residual, (residual_stream, norm_output, query_rows, key_rows, value_rows, result_output, log_sum_exp, preactivation, activation_value))

def backward_layer(grad_resid, params, keep_mask, cosine, sine, allowed):
    gain_vectors, shift_vectors, qkv_w, qkv_b, dense_w, dense_b, in_w, in_b, out_w, out_b = params
    residual_stream, norm_output, query_rows, key_rows, value_rows, result_output, log_sum_exp, preactivation, activation_value = keep_mask
    count = residual_stream.shape[0]
    branch_bias = lax.optimization_barrier(jnp.sum(grad_resid, axis=0))
    grad_low = grad_resid.astype(jnp.bfloat16)
    out_w_grad = jnp.dot(activation_value.T, grad_low, preferred_element_type=jnp.float32)
    act_grad = jnp.dot(grad_low, out_w.T, preferred_element_type=jnp.float32)
    pre_grad = act_grad * gelu_slope(preactivation)
    pre_low = pre_grad.astype(jnp.bfloat16)
    in_w_grad = jnp.dot(norm_output[1].T, pre_low, preferred_element_type=jnp.float32)
    in_b_grad = lax.optimization_barrier(jnp.sum(pre_grad, axis=0)).reshape(in_b.shape)
    second_grad = jnp.dot(pre_low, in_w.T, preferred_element_type=jnp.float32)
    flat = result_output.reshape(count, D)
    dense_w_grad = jnp.dot(flat.T, grad_low, preferred_element_type=jnp.float32)
    out_grad = jnp.dot(grad_low, dense_w.T, preferred_element_type=jnp.float32).astype(jnp.bfloat16).reshape(result_output.shape)
    query_grad, key_grad, value_grad = attend_back(query_rows, key_rows, value_rows, result_output, log_sum_exp, out_grad, allowed)
    query_grad = rotate(query_grad.reshape(count, H, HD), cosine, sine, -1.0)
    key_grad = rotate(key_grad.reshape(count, H, HD), cosine, sine, -1.0)
    value_grad = value_grad.reshape(count, H, HD)
    proj_grad = jnp.stack([query_grad, key_grad, value_grad]).reshape(3, count, D)
    qkv_b_grad = lax.optimization_barrier(jnp.sum(proj_grad, axis=1)).reshape(qkv_b.shape)
    proj_low = proj_grad.astype(jnp.bfloat16)
    qkv_w_grad = jnp.stack([jnp.dot(norm_output[0].T, proj_low[part], preferred_element_type=jnp.float32) for part in range(3)])
    first_grad = jnp.dot(proj_low[0], qkv_w[0].T, preferred_element_type=jnp.float32)
    first_grad = first_grad + jnp.dot(proj_low[1], qkv_w[1].T, preferred_element_type=jnp.float32)
    first_grad = first_grad + jnp.dot(proj_low[2], qkv_w[2].T, preferred_element_type=jnp.float32)
    norm_gradients = jnp.stack([first_grad, second_grad])
    centered_scaled, reciprocal_deviation = apply_layer_norm(residual_stream)
    gain_gradient = lax.optimization_barrier(jnp.sum(norm_gradients * centered_scaled[None], axis=1))
    shift_grad = lax.optimization_barrier(jnp.sum(norm_gradients, axis=1))
    centered_gradient = lax.optimization_barrier(jnp.sum(norm_gradients * gain_vectors.astype(jnp.float32)[:, None, :], axis=0))
    inner_hidden = centered_gradient - lax.optimization_barrier(jnp.mean(centered_gradient, axis=-1, keepdims=True)) - centered_scaled * lax.optimization_barrier(jnp.mean(centered_gradient * centered_scaled, axis=-1, keepdims=True))
    new_grad = grad_resid + reciprocal_deviation * inner_hidden
    return (new_grad, (gain_gradient, shift_grad, qkv_w_grad, qkv_b_grad, dense_w_grad, branch_bias, in_w_grad, in_b_grad, out_w_grad, branch_bias))

def reference(tokens, cotangent, segments, positions, norm_gain, norm_bias, qkv_weight, qkv_bias, dense_weight, dense_bias, in_weight, in_bias, out_weight, out_bias):
    weights = (norm_gain, norm_bias, qkv_weight, qkv_bias, dense_weight, dense_bias, in_weight, in_bias, out_weight, out_bias)
    group_size = SEQ_DEV * SEQ
    blocks = (tokens.reshape(N_DP, group_size, D), cotangent.reshape(N_DP, group_size, D), segments.reshape(N_DP, group_size), positions.reshape(N_DP, group_size))

    def one_group(totals, block):
        block_tokens, block_cot, block_segs, block_pos = block
        cosine, sine = rope_tables(block_pos)
        allowed = build_allowed(block_segs)
        residual_stream = block_tokens.astype(jnp.float32)
        kept = []
        for layer_index in range(LAYERS):
            params = tuple((array[layer_index] for array in weights))
            residual_stream, keep_mask = forward_layer(residual_stream, params, cosine, sine, allowed)
            kept.append(keep_mask)
        grad_resid = block_cot.astype(jnp.float32)
        layer_grads = [None] * LAYERS
        for layer_index in reversed(range(LAYERS)):
            params = tuple((array[layer_index] for array in weights))
            grad_resid, found = backward_layer(grad_resid, params, kept[layer_index], cosine, sine, allowed)
            layer_grads[layer_index] = found
        stacked = tuple((jnp.stack([found[member] for found in layer_grads]) for member in range(10)))
        totals = tuple((before + after for before, after in zip(totals, stacked)))
        return (totals, (residual_stream.astype(jnp.bfloat16), grad_resid.astype(jnp.bfloat16)))
    init = tuple((jnp.zeros(array.shape, jnp.float32) for array in weights))
    totals, (outputs, input_grads) = lax.scan(one_group, init, blocks)
    return (outputs.reshape(TOKENS, D), input_grads.reshape(TOKENS, D), totals[0], totals[1], totals[2], totals[3], totals[4], totals[5], totals[6], totals[7], totals[8], totals[9])
```

```python
import functools
import math

import jax
import jax.numpy as jnp
from jax import lax
from jax.sharding import PartitionSpec as P

HD = 256
ROT = 64
SEQ = 512

norm_eps = 1e-05
root_half = 0.7071067811865476
inv_root_tau = 0.3989422804014327


F32 = jnp.float32
BF16 = jnp.bfloat16


class Exchange:
    ORDER = (0, 2, 4, 6, 1, 3, 5, 7)

    def __init__(self, n_dp, n_tensor):
        self.n_dp = n_dp
        self.n_tensor = n_tensor
        self.cube = n_dp == 8
        self.line = n_tensor == 4

    def flip(self, value, mask):
        return lax.ppermute(value, "dp", [(i, i ^ mask) for i in range(self.n_dp)])

    def shift(self, value, step):
        n = self.n_tensor
        return lax.ppermute(value, "tensor", [(i, (i + step) % n) for i in range(n)])


    def to_own(self, rows):
        if not self.cube:
            return rows
        me = lax.axis_index("dp")
        width = rows.shape[1] // 8
        return jnp.concatenate(
            [lax.dynamic_slice_in_dim(rows, (me ^ o) * width, width, 1) for o in self.ORDER], axis=1
        )

    def to_natural(self, rows):
        if not self.cube:
            return rows
        me = lax.axis_index("dp")
        width = rows.shape[1] // 8
        parts = []
        for p in range(8):
            mask = me ^ p
            slot = (mask >> 1) | ((mask & 1) << 2)
            parts.append(lax.dynamic_slice_in_dim(rows, slot * width, width, 1))
        return jnp.concatenate(parts, axis=1)

    def swap(self, table):
        if not self.cube:
            return table
        me = lax.axis_index("dp")
        cube = table.reshape(2, 2, 2, -1)
        for axis, bit in ((0, 4), (1, 2), (2, 1)):
            cube = jnp.where((me & bit) != 0, jnp.flip(cube, axis), cube)
        return cube.reshape(table.shape)


    def gather(self, own, axis):
        if not self.cube:
            return lax.all_gather(own, "dp", axis=axis, tiled=True)
        half = own.shape[axis] // 2
        over_x = self.flip(own, 2)
        over_y = self.flip(own, 4)
        low = self.flip(lax.slice_in_dim(over_x, 0, half, axis=axis), 4)
        high = self.flip(lax.slice_in_dim(over_y, half, 2 * half, axis=axis), 2)
        mine = [own, over_x, over_y, low, high]
        other = [self.flip(piece, 1) for piece in mine]
        return jnp.concatenate(mine + other, axis=axis)

    def gather_small(self, vector):
        if not self.cube:
            return lax.all_gather(vector, "dp", axis=0)
        return jnp.stack([vector] + [self.flip(vector, mask) for mask in range(1, 8)])

    def scatter(self, make, axis):
        if not self.cube:
            return lax.psum_scatter(make(None), "dp", scatter_dimension=axis, tiled=True).astype(F32)
        away = self.flip(make(1), 1)
        keep = make(0)
        width = keep.shape[axis] // 4
        half = width // 2

        def part(index, which):
            start = index * width + which * half
            return lax.slice_in_dim(keep, start, start + half, axis=axis).astype(
                F32
            ) + lax.slice_in_dim(away, start, start + half, axis=axis).astype(F32)

        def low(value):
            return value.astype(BF16)

        got_x = [self.flip(low(part(index, 0)), 2) for index in (1, 3)]
        got_y = [self.flip(low(part(index, 1)), 4) for index in (2, 3)]
        last_y = self.flip(low(part(2, 0) + got_x[1].astype(F32)), 4)
        last_x = self.flip(low(part(1, 1) + got_y[1].astype(F32)), 2)
        return jnp.concatenate(
            [
                part(0, 0) + got_x[0].astype(F32) + last_y.astype(F32),
                part(0, 1) + got_y[0].astype(F32) + last_x.astype(F32),
            ],
            axis=axis,
        )

    def scatter_small(self, table):
        if not self.cube:
            return lax.psum_scatter(table, "dp", scatter_dimension=0, tiled=False)
        total = table[0]
        for mask in range(1, 8):
            total = total + self.flip(table[mask], mask)
        return total


    def gather_tokens(self, rows):
        if not self.line:
            return lax.all_gather(rows, "tensor", axis=0, tiled=True)
        return jnp.concatenate([rows] + [self.shift(rows, step) for step in range(1, 4)], axis=0)

    def token_order(self, vector):
        if not self.line:
            return vector
        t = lax.axis_index("tensor")
        width = vector.shape[0] // 4
        return jnp.concatenate(
            [lax.dynamic_slice_in_dim(vector, ((t - b) % 4) * width, width, 0) for b in range(4)]
        )

    def scatter_tokens(self, rows):
        if not self.line:
            return lax.psum_scatter(rows.astype(BF16), "tensor", scatter_dimension=0, tiled=True).astype(F32)
        width = rows.shape[0] // 4
        total = rows[:width]
        for b in range(1, 4):
            total = total + self.shift(
                rows[b * width : (b + 1) * width].astype(BF16), -b
            ).astype(F32)
        return total

    def sum_tensor(self, vector):
        if self.n_tensor & (self.n_tensor - 1):
            return lax.psum(vector, "tensor")
        bit = 1
        while bit < self.n_tensor:
            vector = vector + lax.ppermute(
                vector, "tensor", [(i, i ^ bit) for i in range(self.n_tensor)]
            )
            bit *= 2
        return vector


def rope_tables(positions):
    half_rot = ROT // 2
    freq = jnp.exp(jnp.arange(half_rot, dtype=F32) * (-2.0 * math.log(10000.0) / ROT))
    angle = positions.astype(F32)[:, None] * freq[None, :]
    return (jnp.cos(angle), jnp.sin(angle))


def rotate(value_rows, cosine, sine, sign):
    half_rot = ROT // 2
    first_half = value_rows[..., :half_rot]
    second_half = value_rows[..., half_rot:ROT]
    cos_wide = cosine[:, None, :]
    sin_wide = sign * sine[:, None, :]
    return jnp.concatenate(
        [
            first_half * cos_wide - second_half * sin_wide,
            second_half * cos_wide + first_half * sin_wide,
            value_rows[..., ROT:],
        ],
        axis=-1,
    )


def layer_norm(rows):
    centred = rows - jnp.mean(rows, axis=-1, keepdims=True)
    rstd = lax.rsqrt(jnp.mean(centred * centred, axis=-1, keepdims=True) + norm_eps)
    return (centred * rstd, rstd)


def gelu(pre):
    return 0.5 * pre * (1.0 + lax.erf(pre * root_half))


def gelu_slope(pre):
    return 0.5 * (1.0 + lax.erf(pre * root_half)) + pre * jnp.exp(-0.5 * pre * pre) * inv_root_tau


def dot(a, b, contract, out=F32):
    return lax.dot_general(a, b, (contract, ((), ())), preferred_element_type=F32).astype(out)


def per_device(
    ex,
    tokens,
    cotangent,
    segments,
    positions,
    norm_gain,
    norm_bias,
    qkv_weight,
    qkv_bias,
    dense_weight,
    dense_bias,
    in_weight,
    in_bias,
    out_weight,
    out_bias,
):
    n_dp = ex.n_dp
    in_w = ex.gather(in_weight[0], 0)
    qkv_w = ex.gather(qkv_weight[0], 1)
    out_w = ex.gather(out_weight[0], 1)
    dense_w = ex.gather(dense_weight[0], 1)

    piece = norm_gain.shape[2]
    ff_rows, ff_piece = in_bias.shape[1:]
    heads, head_piece = qkv_bias.shape[2:]
    feature = jnp.concatenate([norm_gain[0], norm_bias[0], dense_bias, out_bias], axis=0)
    packed = jnp.concatenate([feature.reshape(-1), in_bias.reshape(-1), qkv_bias.reshape(-1)])
    n_feature = feature.size
    n_ff = in_bias.size
    table = ex.gather_small(packed)
    order = list(ex.ORDER) if ex.cube else list(range(n_dp))
    vectors = (
        jnp.stack([table[o, :n_feature].reshape(6, piece) for o in order], axis=1)
        .reshape(6, n_dp * piece)
        .astype(F32)
    )
    gain_a, gain_m, bias_a, bias_m, dense_b, out_b = (vectors[i] for i in range(6))
    other = ex.swap(table[:, n_feature:])
    in_b = other[:, :n_ff].reshape(n_dp, ff_rows, ff_piece).transpose(1, 0, 2).reshape(-1).astype(F32)
    qkv_b = (
        other[:, n_ff:]
        .reshape(n_dp, 3, heads, head_piece)
        .transpose(1, 2, 0, 3)
        .reshape(3, heads * n_dp * head_piece)
        .astype(F32)
    )

    own_tokens = ex.to_own(tokens)
    own_cot = ex.to_own(cotangent)
    rows = ex.gather_tokens(own_tokens).astype(F32)
    grad = ex.gather_tokens(own_cot)
    count = rows.shape[0]
    groups = count // SEQ
    xhat, rstd = layer_norm(rows)
    normed_a = (xhat * gain_a + bias_a).astype(BF16)
    normed_m = (xhat * gain_m + bias_m).astype(BF16)

    cosine, sine = rope_tables(ex.token_order(positions))
    segs = ex.token_order(segments).reshape(groups, SEQ)
    place = ex.token_order(jnp.arange(count, dtype=jnp.int32)).reshape(groups, SEQ)
    allowed = (segs[:, :, None] == segs[:, None, :]) & (place[:, :, None] >= place[:, None, :])

    pre = dot(normed_m, in_w, ((1,), (0,))) + in_b
    act = gelu(pre).astype(BF16)

    half_d = grad.shape[1] // 2

    def columns(array, which):
        return array if which is None else array[:, which * half_d : (which + 1) * half_d]

    out_w_grad = ex.scatter(lambda w: dot(act, columns(grad, w), ((0,), (0,)), BF16), 1)

    scaling = 1.0 / math.sqrt(HD)
    proj = jnp.einsum("td,jde->jte", normed_a, qkv_w, preferred_element_type=F32) + qkv_b[:, None, :]
    shaped = proj.reshape(3, count, heads, HD)
    query = rotate(shaped[0], cosine, sine, 1.0).astype(BF16).reshape(groups, SEQ, heads, HD)
    keys = rotate(shaped[1], cosine, sine, 1.0).astype(BF16).reshape(groups, SEQ, heads, HD)
    values = shaped[2].astype(BF16).reshape(groups, SEQ, heads, HD)
    scores = jnp.einsum("sqhd,skhd->shqk", query, keys, preferred_element_type=F32) * scaling
    scores = jnp.where(allowed[:, None], scores, -1e30)
    top = jnp.max(scores, axis=-1, keepdims=True)
    expo = jnp.exp(scores - top)
    total = jnp.sum(expo, axis=-1, keepdims=True)
    probs = expo / total
    probs_low = probs.astype(BF16)
    attn = jnp.einsum("shqk,skhd->sqhd", probs_low, values, preferred_element_type=F32).astype(BF16)
    flat = attn.reshape(count, heads * HD)

    dense_w_grad = ex.scatter(lambda w: dot(flat, columns(grad, w), ((0,), (0,)), BF16), 1)

    act_grad = dot(grad, out_w, ((1,), (1,)))
    pre_grad = act_grad * gelu_slope(pre)
    pre_low = pre_grad.astype(BF16)
    in_b_grad = jnp.sum(pre_grad, axis=0)
    in_w_grad = ex.scatter(lambda w: dot(columns(normed_m, w), pre_low, ((0,), (0,)), BF16), 0)
    second = dot(pre_low, in_w, ((1,), (1,)))

    branch = dot(flat, dense_w, ((1,), (0,))) + dot(act, out_w, ((1,), (0,)))
    layer_out = own_tokens.astype(F32) + ex.scatter_tokens(branch) + dense_b + out_b

    out_grad = dot(grad, dense_w, ((1,), (1,)), BF16).reshape(attn.shape)
    value_grad = jnp.einsum("shqk,sqhd->skhd", probs_low, out_grad, preferred_element_type=F32)
    prob_grad = jnp.einsum("sqhd,skhd->shqk", out_grad, values, preferred_element_type=F32)
    delta = jnp.einsum("sqhd,sqhd->shq", out_grad, attn, preferred_element_type=F32)
    score_grad = (probs * (prob_grad - delta[..., None])).astype(BF16)
    query_grad = jnp.einsum("shqk,skhd->sqhd", score_grad, keys, preferred_element_type=F32) * scaling
    key_grad = jnp.einsum("shqk,sqhd->skhd", score_grad, query, preferred_element_type=F32) * scaling
    query_grad = rotate(query_grad.reshape(count, heads, HD), cosine, sine, -1.0)
    key_grad = rotate(key_grad.reshape(count, heads, HD), cosine, sine, -1.0)
    value_grad = value_grad.reshape(count, heads, HD)
    proj_grad = jnp.stack([query_grad, key_grad, value_grad]).reshape(3, count, heads * HD)
    qkv_b_grad = jnp.sum(proj_grad, axis=1)
    proj_low = proj_grad.astype(BF16)
    qkv_w_grad = ex.scatter(
        lambda w: jnp.einsum(
            "td,jte->jde", columns(normed_a, w), proj_low, preferred_element_type=F32
        ).astype(BF16),
        1,
    )
    first = jnp.einsum("jte,jde->td", proj_low, qkv_w, preferred_element_type=F32)

    hidden = ex.scatter_tokens(first * gain_a + second * gain_m)
    own_xhat, own_rstd = layer_norm(own_tokens.astype(F32))
    inner = (
        hidden
        - jnp.mean(hidden, axis=-1, keepdims=True)
        - own_xhat * jnp.mean(hidden * own_xhat, axis=-1, keepdims=True)
    )
    tokens_grad = own_cot.astype(F32) + own_rstd * inner

    feature_grads = jnp.stack(
        [
            jnp.sum(first * xhat, axis=0),
            jnp.sum(second * xhat, axis=0),
            jnp.sum(first, axis=0),
            jnp.sum(second, axis=0),
            jnp.sum(own_cot.astype(F32), axis=0),
        ]
    ).reshape(5, n_dp, piece)
    spots = [order.index(mask) for mask in range(n_dp)]
    feature_table = jnp.stack([feature_grads[:, spot].reshape(-1) for spot in spots])
    in_b_table = in_b_grad.reshape(ff_rows, n_dp, ff_piece).transpose(1, 0, 2).reshape(n_dp, -1)
    qkv_b_table = (
        qkv_b_grad.reshape(3, heads, n_dp, head_piece).transpose(2, 0, 1, 3).reshape(n_dp, -1)
    )
    other_table = ex.swap(jnp.concatenate([in_b_table, qkv_b_table], axis=1))
    sums = ex.scatter_small(jnp.concatenate([feature_table, other_table], axis=1))
    n_sums = 5 * piece
    feature_sums = ex.sum_tensor(sums[:n_sums]).reshape(5, piece)
    in_b_sum = sums[n_sums : n_sums + n_ff].reshape(in_bias.shape)
    qkv_b_sum = sums[n_sums + n_ff :].reshape(qkv_bias.shape)
    bias_sum = feature_sums[4:5]
    return (
        ex.to_natural(layer_out.astype(BF16)),
        ex.to_natural(tokens_grad.astype(BF16)),
        feature_sums[None, 0:2],
        feature_sums[None, 2:4],
        qkv_w_grad[None],
        qkv_b_sum,
        dense_w_grad[None],
        bias_sum,
        in_w_grad[None],
        in_b_sum,
        out_w_grad[None],
        bias_sum,
    )


def solution(mesh):
    tokens = P(("dp", "tensor"), None)
    group = P("dp")
    norm = P(None, None, "dp")
    column = P(None, "dp", "tensor")
    row = P(None, "tensor", "dp")
    bias = P(None, "dp")
    qkv = P(None, None, "dp", "tensor")
    qkv_b = P(None, None, "tensor", "dp")
    params = (norm, norm, qkv, qkv_b, row, bias, column, row, row, bias)
    ex = Exchange(mesh.shape["dp"], mesh.shape["tensor"])
    return jax.shard_map(
        functools.partial(per_device, ex),
        mesh=mesh,
        in_specs=(tokens, tokens, group, group) + params,
        out_specs=(tokens, tokens) + params,
        check_vma=False,
    )
```
